32 devices in a mesh: gx: 4 (over z), gy: 4 (over y, core), gz: 2 (over x).
Axes of the slice: x: 2, y: 2, z: 4, core: 2. Of those that a mesh axis runs over, the one named last changes fastest.
Arguments:
- source: float32 [32, 64, 512], P('gx', 'gy', 'gz'), may hold values from -4 to 4
- conduct: float32 [32, 64, 512], P('gx', 'gy', 'gz'), may hold values from 0.5 to 2
- solid_mask: int32 [32, 64, 512], P('gx', 'gy', 'gz'), may hold values 0 or 1
- line_ids: int32 [4, 4, 2, 16], P('gx', 'gy'), may hold values from -1 to 31, as said below
Outputs:
- pressure: float32 [32, 64, 512], P('gx', 'gy', 'gz')
The draws below stay inside these ranges and needn't reach their ends.
Inputs may be any that keep to these rules, and one draw needn't show every extreme that they name: Entries of line_ids[g, h, o, :] are numbers a * 8 + b of coarse columns (coarse cells [a, b, :] of every device with gx index g and gy index h), padded at the end with -1; no column is listed twice for one (g, h); every owner o lists at least one, and for every (g, h) some owner fills all 16 slots.
All inputs are finite; a program needn't handle non-finite values. No bound on the sum of `solid_mask` on one device may be relied on, other than what follows from the above.
Results may differ from the reference program's by a relative error of at most 0.00055.
Values sent between devices are 32-bit elements; how exact they have to be, the bound alone decides.
A program may use at most 64 MiB of HBM per device.

```python
import math
import jax
import jax.numpy as jnp
from jax import lax

CX = 8
CY = 16
CZ = 256
SWEEPS = 2
NX = 32
NY = 64
NZ = 512
LINES = 32
CAP = 16
N_GX = 4
N_GY = 4
N_GZ = 2


def draw_source(key, part):
    return jax.random.truncated_normal(key, -4.0, 4.0, (NX, NY, NZ), jnp.float32)


def draw_line_ids(key, part):
    columns = N_GX * N_GY
    subkeys = jax.random.split(key, 3)
    column_keys = jax.random.split(subkeys[0], columns)
    orders = jax.vmap(lambda column_key: jax.random.permutation(column_key, LINES))(column_keys)
    counts = jax.random.randint(subkeys[1], (columns, N_GZ), 1, CAP + 1)
    fullest = jax.random.randint(subkeys[2], (columns,), 0, N_GZ)
    owner_index = jnp.arange(N_GZ, dtype=jnp.int32)
    counts = jnp.where(owner_index[None, :] == fullest[:, None], CAP, counts)
    starts = jnp.cumsum(counts, axis=1) - counts
    slot_index = jnp.arange(CAP, dtype=jnp.int32)
    position = starts[:, :, None] + slot_index[None, None, :]
    is_valid = slot_index[None, None, :] < counts[:, :, None]
    position = jnp.minimum(position, LINES - 1).reshape(columns, N_GZ * CAP)
    chosen = jnp.take_along_axis(orders, position, axis=1).reshape(columns, N_GZ, CAP)
    chosen = jnp.where(is_valid, chosen, -1)
    return chosen.reshape(N_GX, N_GY, N_GZ, CAP).astype(jnp.int32)


def plant(values, rng, smallest, largest):
    place = [jax.random.randint(jax.random.fold_in(rng, axis), (), 0, length) for axis, length in enumerate(values.shape)]
    longest = values.shape.index(max(values.shape))
    next_to = place[:longest] + [(place[longest] + 1) % values.shape[longest]] + place[longest + 1:]
    return values.at[tuple(place)].set(smallest).at[tuple(next_to)].set(largest)


def shard_levels(key, dims, pieces, least, high):
    loudness, own = 1.0, jax.random.fold_in(key, 6)
    for axis_at, parts in pieces:
        draws = jnp.exp(jax.random.uniform(jax.random.fold_in(own, axis_at), (parts,), jnp.float32, least / len(pieces), high / len(pieces)))
        loudness = loudness * jnp.repeat(draws, dims[axis_at] // parts).reshape([-1 if axis == axis_at else 1 for axis in range(len(dims))])
    return loudness


def setup_inputs(seed: int = 0) -> dict:
    streams_of = jax.random.split(jax.random.key(seed), 5)
    source = draw_source(jax.random.fold_in(streams_of[4], 71), 0)
    conduct = jnp.clip(jnp.exp(math.log(2.0) - 1.3862944 * jax.random.uniform(streams_of[1], (NX, NY, NZ), jnp.float32) ** shard_levels(streams_of[1], (NX, NY, NZ), ((0, 4), (1, 4), (2, 2)), -0.2, 0.2)), 0.5, 2.0)
    solid_mask = plant((jax.random.randint(streams_of[2], (NX, NY, NZ), 0, 10) < 3).astype(jnp.int32), jax.random.fold_in(streams_of[2], 1), 0, 1)
    line_ids = draw_line_ids(jax.random.fold_in(streams_of[4], 71), 0)
    return {"source": source, "conduct": conduct, "solid_mask": solid_mask, "line_ids": line_ids}


clog_factor = 0.2
shift_fine = 0.001

def neighbours(padded):
    return [padded[2:, 1:-1, 1:-1], padded[:-2, 1:-1, 1:-1], padded[1:-1, 2:, 1:-1], padded[1:-1, :-2, 1:-1], padded[1:-1, 1:-1, 2:], padded[1:-1, 1:-1, :-2]]

def face_weights(padded_cond):
    centre = padded_cond[1:-1, 1:-1, 1:-1]
    weights = [0.5 * (centre + beside) for beside in neighbours(padded_cond)]
    diagonal = shift_fine + weights[0] + weights[1] + weights[2] + weights[3] + weights[4] + weights[5]
    return (weights, diagonal)

def inflow_of(padded, weights):
    besides = neighbours(padded)
    inflow = weights[0] * besides[0]
    for weight, beside in zip(weights[1:], besides[1:]):
        inflow = inflow + weight * beside
    return inflow

def parity_of(extent, offset):
    along_x = jnp.arange(extent[0], dtype=jnp.int32)[:, None, None]
    along_y = jnp.arange(extent[1], dtype=jnp.int32)[None, :, None]
    along_z = jnp.arange(extent[2], dtype=jnp.int32)[None, None, :]
    return (along_x + along_y + along_z + offset) % 2

def block_mean(values):
    extent = values.shape
    return values.reshape(extent[0] // 2, 2, extent[1] // 2, 2, extent[2] // 2, 2).mean(axis=(1, 3, 5))

def prolong(coarse):
    return jnp.repeat(jnp.repeat(jnp.repeat(coarse, 2, axis=0), 2, axis=1), 2, axis=2)

def line_solve(line_rhs, line_cond):
    screen = 1.0 / (CZ * CZ)
    pair_sums = line_cond[..., :-1] + line_cond[..., 1:]
    left_sum = jnp.concatenate([line_cond[..., :1], pair_sums], axis=-1)
    right_sum = jnp.concatenate([pair_sums, line_cond[..., -1:]], axis=-1)
    main_diag = screen + left_sum + right_sum
    zero_col = jnp.zeros_like(line_cond[..., :1])
    lower_diag = jnp.concatenate([zero_col, -pair_sums], axis=-1)
    upper_diag = jnp.concatenate([-pair_sums, zero_col], axis=-1)
    solved = lax.linalg.tridiagonal_solve(lower_diag, main_diag, upper_diag, line_rhs[..., None])
    return solved[..., 0]

def red_black(pressure, source, weights, diagonal, colours):
    for colour in (0, 1):
        updated = (source + inflow_of(jnp.pad(pressure, 1), weights)) / diagonal
        pressure = jnp.where(colours == colour, updated, pressure)
    return pressure

def reference(source, conduct, solid_mask, line_ids):
    relax_weight = 2.0 / (CZ * CZ)
    clogged = conduct * jnp.where(solid_mask > 0, clog_factor, 1.0)
    weights, diagonal = face_weights(jnp.pad(clogged, 1))
    colours = parity_of(source.shape, 0)
    pressure = jnp.zeros_like(source)
    for sweep_no in range(SWEEPS):
        pressure = red_black(pressure, source, weights, diagonal, colours)
    residual = source - (diagonal * pressure - inflow_of(jnp.pad(pressure, 1), weights))
    coarse_rhs = block_mean(residual)
    coarse_cond = block_mean(clogged)
    slot_ids = line_ids.reshape(N_GX, N_GY, N_GZ * CAP).astype(jnp.int32)
    is_valid = slot_ids >= 0
    coarse_row = jnp.arange(N_GX, dtype=jnp.int32)[:, None, None] * (CX // 2) + slot_ids // (CY // 2)
    coarse_col = jnp.arange(N_GY, dtype=jnp.int32)[None, :, None] * (CY // 2) + slot_ids % (CY // 2)
    flat_index = jnp.where(is_valid, coarse_row * (NY // 2) + coarse_col, 0).astype(jnp.int32)
    flagged = jnp.zeros((NX // 2 * (NY // 2),), coarse_rhs.dtype)
    flagged = flagged.at[flat_index.reshape(-1)].max(is_valid.reshape(-1).astype(coarse_rhs.dtype))
    flagged = flagged.reshape(NX // 2, NY // 2)[:, :, None]
    correction = line_solve(coarse_rhs * flagged, coarse_cond * flagged)
    pressure = pressure + relax_weight * prolong(correction)
    for sweep_no in range(SWEEPS):
        pressure = red_black(pressure, source, weights, diagonal, colours)
    return pressure
```

```python
import functools

import jax
import jax.numpy as jnp
from jax import lax
from jax.experimental import pallas as pl
from jax.experimental.pallas import tpu as pltpu
from jax.sharding import PartitionSpec as P

CZ = 256
ROUNDS = 9
clog_factor = 0.2
shift_fine = 0.001
MESH = pl.DeviceIdType.MESH
AXES = ("gx", "gy", "gz")


def split3(x):
    hi = x.astype(jnp.bfloat16)
    rest = x - hi.astype(jnp.float32)
    mid = rest.astype(jnp.bfloat16)
    low = (rest - mid.astype(jnp.float32)).astype(jnp.bfloat16)
    return jnp.concatenate([hi, mid, low], axis=0)


def exact_dot(x, ones):
    rows = x.shape[0]
    y = jnp.dot(split3(x), ones, preferred_element_type=jnp.float32)
    return (y[2 * rows :] + y[rows : 2 * rows]) + y[:rows]


def kernel(
    sizes,
    src_hbm,
    con_hbm,
    msk_hbm,
    ids_hbm,
    out_ref,
    src,
    con,
    msk,
    ids,
    hx,
    hy,
    hz,
    sx,
    sy,
    sz,
    wx,
    wyi,
    wzi,
    wyh,
    wzh,
    diag,
    srd,
    tmp,
    pool_m,
    prol_m,
    cond_all,
    rhs_all,
    cond_send,
    rhs_send,
    fac,
    in_sem,
    send_sem,
    recv_sem,
    g_send,
    g_recv,
):
    X, Y, Z = src.shape
    ZC = Z // 2
    here = [lax.axis_index(a) for a in AXES]
    n_gz = sizes[2]
    length = n_gz * ZC
    stages = (length - 1).bit_length()

    loads = [
        pltpu.make_async_copy(a, b, in_sem.at[i])
        for i, (a, b) in enumerate(
            ((con_hbm, con), (msk_hbm, msk), (src_hbm, src), (ids_hbm, ids))
        )
    ]
    for load in loads:
        load.start()

    halo = (hx, hy, hz)
    outgoing = (sx, sy, sz)
    has = [
        (here[d] > 0, here[d] < sizes[d] - 1) for d in range(3)
    ]

    for d in range(3):
        for side in range(2):

            @pl.when(jnp.logical_not(has[d][side]))
            def _():
                for r in range(ROUNDS):
                    halo[d][r, side] = jnp.zeros(halo[d].shape[2:], jnp.float32)

    barrier = pltpu.get_barrier_semaphore()
    for d in range(2):
        for side in range(2):

            @pl.when(has[d][side])
            def _():
                pl.semaphore_signal(
                    barrier,
                    inc=1,
                    device_id={AXES[d]: here[d] + (2 * side - 1)},
                    device_id_type=MESH,
                )

    for off in range(1, n_gz):
        pl.semaphore_signal(
            barrier,
            inc=1,
            device_id={"gz": lax.rem(here[2] + off, n_gz)},
            device_id_type=MESH,
        )

    def face_copy(r, d, side):
        return pltpu.make_async_remote_copy(
            src_ref=outgoing[d].at[r, side],
            dst_ref=halo[d].at[r, 1 - side],
            send_sem=send_sem.at[r, d, side],
            recv_sem=recv_sem.at[r, d, 1 - side],
            device_id={AXES[d]: here[d] + (2 * side - 1)},
            device_id_type=MESH,
        )

    def face_arrival(r, d, side):
        return pltpu.make_async_remote_copy(
            src_ref=outgoing[d].at[r, side],
            dst_ref=halo[d].at[r, side],
            send_sem=send_sem.at[r, d, side],
            recv_sem=recv_sem.at[r, d, side],
            device_id={AXES[d]: here[d] + (2 * side - 1)},
            device_id_type=MESH,
        )

    lane = lax.broadcasted_iota(jnp.int32, (Y, 128), 1)

    def pack(p, side):
        at = Z - 1 if side else 0
        acc = jnp.broadcast_to(p[0, :, at : at + 1], (Y, 128))
        for x in range(1, X):
            acc = jnp.where(lane == x, jnp.broadcast_to(p[x, :, at : at + 1], (Y, 128)), acc)
        return acc

    def stage_faces(r, p):
        sx[r, 0] = p[0]
        sx[r, 1] = p[X - 1]
        sy[r, 0] = p[:, 0:1, :]
        sy[r, 1] = p[:, Y - 1 : Y, :]
        for side in range(2):

            @pl.when(has[2][side])
            def _():
                sz[r, side] = pack(p, side)

    def start_faces(r):
        for d in (2, 0, 1):
            for side in range(2):

                @pl.when(has[d][side])
                def _():
                    face_copy(r, d, side).start()

    def wait_faces(r):
        for d in range(3):
            for side in range(2):

                @pl.when(has[d][side])
                def _():
                    face_arrival(r, d, side).wait_recv()

    def send_faces(r, p):
        stage_faces(r, p)
        start_faces(r)

    def z_halo(r, side):
        packed = hz[r, side]
        return jnp.stack(
            [jnp.broadcast_to(packed[:, x : x + 1], (Y, 128)) for x in range(X)], axis=0
        )

    def gather_copy(buf, staged, which, off):
        return pltpu.make_async_remote_copy(
            src_ref=staged,
            dst_ref=buf.at[here[2]],
            send_sem=g_send.at[which, off - 1],
            recv_sem=g_recv.at[which, off - 1],
            device_id={"gz": lax.rem(here[2] + off, n_gz)},
            device_id_type=MESH,
        )

    def gather_start(buf, staged, which, value):
        staged[...] = value
        for off in range(1, n_gz):
            gather_copy(buf, staged, which, off).start()
        buf[here[2]] = value

    def gather_wait(buf, staged, which):
        for off in range(1, n_gz):
            gather_copy(buf, staged, which, off).wait_recv()
        return jnp.concatenate([buf[j] for j in range(n_gz)], axis=1)

    def pool(v):
        for h in range(2):
            part = v[:, :, 128 * h : 128 * h + 128].reshape(X // 2, 2, Y, 128)
            tmp[h] = (part[:, 0] + part[:, 1]).reshape(X // 2 * Y, 128)
        rows = X // 2 * Y // 2
        halves = [
            tmp[h, pl.ds(0, rows, stride=2), :] + tmp[h, pl.ds(1, rows, stride=2), :]
            for h in range(2)
        ]
        return exact_dot(jnp.concatenate(halves, axis=1), pool_m[...]) * 0.125

    loads[0].wait()
    loads[1].wait()
    c = con[...] * jnp.where(msk[...] > 0, clog_factor, 1.0)
    stage_faces(0, c)
    greeted = n_gz - 1
    for d in range(2):
        greeted = greeted + has[d][0].astype(jnp.int32) + has[d][1].astype(jnp.int32)
    pl.semaphore_wait(barrier, greeted)
    start_faces(0)

    k_of = lax.broadcasted_iota(jnp.int32, (Z, ZC), 0)
    j_of = lax.broadcasted_iota(jnp.int32, (Z, ZC), 1)
    pool_m[...] = jnp.where((k_of >> 1) == j_of, 1.0, 0.0).astype(jnp.bfloat16)
    k_of = lax.broadcasted_iota(jnp.int32, (ZC, Z), 1)
    j_of = lax.broadcasted_iota(jnp.int32, (ZC, Z), 0)
    prol_m[...] = jnp.where((k_of >> 1) == j_of, 1.0, 0.0).astype(jnp.bfloat16)
    gather_start(cond_all, cond_send, 0, pool(c))

    iy = lax.broadcasted_iota(jnp.int32, (X, Y, Z), 1)
    iz = lax.broadcasted_iota(jnp.int32, (X, Y, Z), 2)
    ix = lax.broadcasted_iota(jnp.int32, (X, Y, Z), 0)
    red = ((ix + iy + iz) & 1) == 0

    loads[2].wait()
    loads[3].wait()
    rows = X // 2 * Y // 2
    col = lax.broadcasted_iota(jnp.int32, (rows, ids.shape[3]), 0)
    hit = jnp.zeros((rows, ids.shape[3]), jnp.float32)
    for o in range(ids.shape[2]):
        hit = jnp.maximum(hit, jnp.where(ids[0, 0, o : o + 1, :] == col, 1.0, 0.0))
    flag = jnp.max(hit, axis=1, keepdims=True)

    wait_faces(0)
    xm = jnp.concatenate([hx[0, 0][None], c[:-1]], axis=0)
    xp = jnp.concatenate([c[1:], hx[0, 1][None]], axis=0)
    ym = jnp.where(iy == 0, jnp.broadcast_to(hy[0, 0], c.shape), pltpu.roll(c, 1, 1))
    yp = jnp.where(iy == Y - 1, jnp.broadcast_to(hy[0, 1], c.shape), pltpu.roll(c, Y - 1, 1))
    h0 = z_halo(0, 0)
    h1 = z_halo(0, 1)
    zm = jnp.where(iz == 0, jnp.concatenate([h0, h0], axis=2), pltpu.roll(c, 1, 2))
    zp = jnp.where(iz == Z - 1, jnp.concatenate([h1, h1], axis=2), pltpu.roll(c, Z - 1, 2))
    w = [0.5 * (c + beside) for beside in (xp, xm, yp, ym, zp, zm)]
    dg = shift_fine + w[0] + w[1] + w[2] + w[3] + w[4] + w[5]
    rd = 1.0 / dg
    s_rd = src[...] * rd
    p = jnp.where(red, s_rd, 0.0)
    send_faces(1, p)
    diag[...] = dg
    srd[...] = s_rd
    w = [one * rd for one in w]
    wx[0] = w[1]
    wx[1] = w[0]
    wyi[0] = jnp.where(iy == 0, 0.0, w[3])
    wyi[1] = jnp.where(iy == Y - 1, 0.0, w[2])
    wzi[0] = jnp.where(iz == 0, 0.0, w[5])
    wzi[1] = jnp.where(iz == Z - 1, 0.0, w[4])
    wyh[0] = jnp.where(iy == 0, w[3], 0.0)[:, :8]
    wyh[1] = jnp.where(iy == Y - 1, w[2], 0.0)[:, Y - 8 :]
    wzh[0] = jnp.where(iz == 0, w[5], 0.0)[:, :, :128]
    wzh[1] = jnp.where(iz == Z - 1, w[4], 0.0)[:, :, Z - 128 :]

    def interior(p):
        plane = jnp.zeros((1,) + p.shape[1:], jnp.float32)
        u = srd[...] + wx[0] * jnp.concatenate([plane, p[:-1]], axis=0)
        u = u + wx[1] * jnp.concatenate([p[1:], plane], axis=0)
        u = u + wyi[0] * pltpu.roll(p, 1, 1) + wyi[1] * pltpu.roll(p, Y - 1, 1)
        u = u + wzi[0] * pltpu.roll(p, 1, 2) + wzi[1] * pltpu.roll(p, Z - 1, 2)
        return u

    def with_halo(r, u):
        wait_faces(r)
        u = jnp.concatenate(
            [
                (u[0] + wx[0, 0] * hx[r, 0])[None],
                u[1:-1],
                (u[X - 1] + wx[1, X - 1] * hx[r, 1])[None],
            ],
            axis=0,
        )
        near = u[:, :8] + wyh[0] * jnp.broadcast_to(hy[r, 0], (X, 8, Z))
        far = u[:, Y - 8 :] + wyh[1] * jnp.broadcast_to(hy[r, 1], (X, 8, Z))
        u = jnp.concatenate([near, u[:, 8 : Y - 8], far] if Y > 16 else [near, far], axis=1)
        left = u[:, :, :128] + wzh[0] * z_halo(r, 0)
        right = u[:, :, Z - 128 :] + wzh[1] * z_halo(r, 1)
        return jnp.concatenate([left, right], axis=2)

    def factor(state, stage):
        lower, main, upper = state
        stride = 1 << stage
        rm = 1.0 / main
        low = -lower * pltpu.roll(rm, stride, 1)
        high = -upper * pltpu.roll(rm, length - stride, 1)
        fac[2 * stage] = low
        fac[2 * stage + 1] = high
        main = (
            main + low * pltpu.roll(upper, stride, 1) + high * pltpu.roll(lower, length - stride, 1)
        )
        lower = low * pltpu.roll(lower, stride, 1)
        upper = high * pltpu.roll(upper, length - stride, 1)
        return lower, main, upper

    u = interior(p)
    cond = gather_wait(cond_all, cond_send, 0)
    at = lax.broadcasted_iota(jnp.int32, cond.shape, 1)
    before = cond + pltpu.roll(cond, 1, 1)
    after = cond + pltpu.roll(cond, length - 1, 1)
    left_sum = jnp.where(at == 0, cond, before)
    right_sum = jnp.where(at == length - 1, cond, after)
    state = (
        jnp.where(at == 0, 0.0, -before),
        1.0 / (CZ * CZ) + left_sum + right_sum,
        jnp.where(at == length - 1, 0.0, -after),
    )
    per = -(-stages // 3)
    for stage in range(0, per):
        state = factor(state, stage)
    p = jnp.where(red, p, with_halo(1, u))
    send_faces(2, p)
    u = interior(p)
    for stage in range(per, min(2 * per, stages)):
        state = factor(state, stage)
    p = jnp.where(red, with_halo(2, u), p)
    send_faces(3, p)
    u = interior(p)
    for stage in range(2 * per, stages):
        state = factor(state, stage)
    fac[2 * stages] = (2.0 / (CZ * CZ)) / state[1]
    p = jnp.where(red, p, with_halo(3, u))
    send_faces(4, p)
    u = with_halo(4, interior(p))
    rhs = pool(diag[...] * (u - p)) * flag
    gather_start(rhs_all, rhs_send, 1, rhs)
    values = gather_wait(rhs_all, rhs_send, 1)
    for stage in range(stages):
        stride = 1 << stage
        values = (
            values
            + fac[2 * stage] * pltpu.roll(values, stride, 1)
            + fac[2 * stage + 1] * pltpu.roll(values, length - stride, 1)
        )
    rhs_all[...] = jnp.stack(
        [
            (values * fac[2 * stages])[:, ZC * j : ZC * j + ZC]
            for j in range(n_gz)
        ],
        axis=0,
    )
    mine = rhs_all[here[2]]
    fine = exact_dot(mine, prol_m[...])
    for h in range(2):
        part = fine[:, 128 * h : 128 * h + 128]
        tmp[h, pl.ds(0, rows, stride=2), :] = part
        tmp[h, pl.ds(1, rows, stride=2), :] = part
    add = jnp.concatenate([tmp[0], tmp[1]], axis=1).reshape(X // 2, 1, Y, Z)
    p = p + jnp.broadcast_to(add, (X // 2, 2, Y, Z)).reshape(X, Y, Z)

    for r in range(5, ROUNDS):
        send_faces(r, p)
        u = with_halo(r, interior(p))
        p = jnp.where(red, u, p) if r % 2 else jnp.where(red, p, u)
    out_ref[...] = p

    for r in range(ROUNDS):
        for d in range(3):
            for side in range(2):

                @pl.when(has[d][side])
                def _():
                    face_copy(r, d, side).wait_send()

    for off in range(1, n_gz):
        gather_copy(cond_all, cond_send, 0, off).wait_send()
        gather_copy(rhs_all, rhs_send, 1, off).wait_send()


def shards(sizes, source, conduct, solid_mask, line_ids):
    X, Y, Z = source.shape
    ZC = Z // 2
    rows = X // 2 * Y // 2
    n_gz = sizes[2]
    length = n_gz * ZC
    stages = (length - 1).bit_length()
    f32 = jnp.float32
    V = pltpu.VMEM
    dma = pltpu.SemaphoreType.DMA
    return pl.pallas_call(
        functools.partial(kernel, sizes),
        out_shape=jax.ShapeDtypeStruct((X, Y, Z), f32),
        in_specs=[pl.BlockSpec(memory_space=pl.ANY)] * 4,
        out_specs=pl.BlockSpec(memory_space=pltpu.VMEM),
        scratch_shapes=[
            V((X, Y, Z), f32),
            V((X, Y, Z), f32),
            V((X, Y, Z), jnp.int32),
            V(line_ids.shape, jnp.int32),
            V((ROUNDS, 2, Y, Z), f32),
            V((ROUNDS, 2, X, 1, Z), f32),
            V((ROUNDS, 2, Y, 128), f32),
            V((ROUNDS, 2, Y, Z), f32),
            V((ROUNDS, 2, X, 1, Z), f32),
            V((ROUNDS, 2, Y, 128), f32),
            V((2, X, Y, Z), f32),
            V((2, X, Y, Z), f32),
            V((2, X, Y, Z), f32),
            V((2, X, 8, Z), f32),
            V((2, X, Y, 128), f32),
            V((X, Y, Z), f32),
            V((X, Y, Z), f32),
            V((2, X // 2 * Y, 128), f32),
            V((Z, ZC), jnp.bfloat16),
            V((ZC, Z), jnp.bfloat16),
            V((n_gz, rows, ZC), f32),
            V((n_gz, rows, ZC), f32),
            V((rows, ZC), f32),
            V((rows, ZC), f32),
            V((2 * stages + 1, rows, length), f32),
            dma((4,)),
            dma((ROUNDS, 3, 2)),
            dma((ROUNDS, 3, 2)),
            dma((2, n_gz - 1)),
            dma((2, n_gz - 1)),
        ],
        compiler_params=pltpu.CompilerParams(
            collective_id=0, has_side_effects=True, vmem_limit_bytes=48 * 1024 * 1024
        ),
        name="cycle",
    )(source, conduct, solid_mask, line_ids)


def solution(mesh):
    sizes = tuple(mesh.shape[a] for a in AXES)
    in_specs = (
        P("gx", "gy", "gz"),
        P("gx", "gy", "gz"),
        P("gx", "gy", "gz"),
        P("gx", "gy", None, None),
    )
    out_specs = P("gx", "gy", "gz")
    return jax.shard_map(
        functools.partial(shards, sizes),
        mesh=mesh,
        in_specs=in_specs,
        out_specs=out_specs,
        check_vma=False,
    )
```

```python
import functools

import jax
import jax.numpy as jnp
from jax import lax
from jax.experimental import pallas as pl
from jax.experimental.pallas import tpu as pltpu
from jax.sharding import PartitionSpec as P

CZ = 256
CHANNELS = 7
EDGES = ((0, 1), (0, 2), (1, 2))
clog_factor = 0.2
shift_fine = 0.001
MESH = pl.DeviceIdType.MESH
AXES = ("gx", "gy", "gz")


def split3(x):
    hi = x.astype(jnp.bfloat16)
    rest = x - hi.astype(jnp.float32)
    mid = rest.astype(jnp.bfloat16)
    low = (rest - mid.astype(jnp.float32)).astype(jnp.bfloat16)
    return jnp.concatenate([hi, mid, low], axis=0)


def exact_dot(x, ones):
    rows = x.shape[0]
    y = jnp.dot(split3(x), ones, preferred_element_type=jnp.float32)
    return (y[2 * rows :] + y[rows : 2 * rows]) + y[:rows]


def kernel(
    sizes,
    src_hbm,
    con_hbm,
    msk_hbm,
    ids_hbm,
    out_ref,
    src,
    con,
    msk,
    ids,
    hx,
    hy,
    hz,
    sx,
    sy,
    sz,
    hxy,
    hxz,
    hyz,
    wts,
    diag,
    srd,
    tmp,
    pool_m,
    prol_m,
    cond_all,
    rhs_all,
    cond_send,
    rhs_send,
    fac,
    in_sem,
    send_sem,
    recv_sem,
    g_send,
    g_recv,
):
    X, Y, Z = src.shape
    ZC = Z // 2
    here = [lax.axis_index(a) for a in AXES]
    n_gz = sizes[2]
    length = n_gz * ZC
    stages = (length - 1).bit_length()

    loads = [
        pltpu.make_async_copy(a, b, in_sem.at[i])
        for i, (a, b) in enumerate(
            ((con_hbm, con), (msk_hbm, msk), (src_hbm, src), (ids_hbm, ids))
        )
    ]
    for load in loads:
        load.start()

    halo = (hx, hy, hz)
    outgoing = (sx, sy, sz)
    edge_halo = (hxy, hxz, hyz)
    has = [(here[d] > 0, here[d] < sizes[d] - 1) for d in range(3)]

    def beside(d, side):
        return {AXES[d]: here[d] + (2 * side - 1)}

    faces = [(d, side) for d in (2, 0, 1) for side in range(2)]
    edges = [(e, a, b) for e in range(3) for a in range(2) for b in range(2)]

    def has_edge(e, a, b):
        return jnp.logical_and(has[EDGES[e][0]][a], has[EDGES[e][1]][b])

    for d, side in faces:

        @pl.when(jnp.logical_not(has[d][side]))
        def _():
            for r in range(CHANNELS):
                halo[d][r, side] = jnp.zeros(halo[d].shape[2:], jnp.float32)

    for e, a, b in edges:

        @pl.when(jnp.logical_not(has_edge(e, a, b)))
        def _():
            for r in (0, 3, 5, 6):
                edge_halo[e][r, a, b] = jnp.zeros(edge_halo[e].shape[3:], jnp.float32)

    barrier = pltpu.get_barrier_semaphore()
    greeted = n_gz - 1
    for d, side in faces:
        if d == 2:
            continue
        greeted = greeted + has[d][side].astype(jnp.int32)

        @pl.when(has[d][side])
        def _():
            pl.semaphore_signal(
                barrier, inc=1, device_id=beside(d, side), device_id_type=MESH
            )

    for e, a, b in edges:
        greeted = greeted + has_edge(e, a, b).astype(jnp.int32)

        @pl.when(has_edge(e, a, b))
        def _():
            pl.semaphore_signal(
                barrier,
                inc=1,
                device_id={**beside(EDGES[e][0], a), **beside(EDGES[e][1], b)},
                device_id_type=MESH,
            )

    for off in range(1, n_gz):
        pl.semaphore_signal(
            barrier,
            inc=1,
            device_id={"gz": lax.rem(here[2] + off, n_gz)},
            device_id_type=MESH,
        )

    def channels_of(ch):
        return pl.ds(0, 3) if ch == 0 else ch

    def face_copy(ch, d, side, parity, arrival=False):
        at = side if arrival else 1 - side
        return pltpu.make_async_remote_copy(
            src_ref=outgoing[d].at[channels_of(ch), side],
            dst_ref=halo[d].at[channels_of(ch), at],
            send_sem=send_sem.at[2 * d + side],
            recv_sem=recv_sem.at[parity, 2 * d + at],
            device_id=beside(d, side),
            device_id_type=MESH,
        )

    def edge_copy(ch, e, a, b, parity, arrival=False):
        to = (a, b) if arrival else (1 - a, 1 - b)
        if e == 0:
            piece = sy.at[ch, b, a * (X - 1)]
        elif e == 1:
            piece = sz.at[ch, b]
        else:
            piece = sz.at[ch, b, pl.ds(a * (Y - 8), 8)]
        return pltpu.make_async_remote_copy(
            src_ref=piece,
            dst_ref=edge_halo[e].at[ch, to[0], to[1]],
            send_sem=send_sem.at[6 + 4 * e + 2 * a + b],
            recv_sem=recv_sem.at[parity, 6 + 4 * e + 2 * to[0] + to[1]],
            device_id={**beside(EDGES[e][0], a), **beside(EDGES[e][1], b)},
            device_id_type=MESH,
        )

    lane = lax.broadcasted_iota(jnp.int32, (Y, 128), 1)
    sub_y = lax.broadcasted_iota(jnp.int32, (X, 8, Z), 1)
    lane_z = lax.broadcasted_iota(jnp.int32, (X, Y, 128), 2)
    iy = lax.broadcasted_iota(jnp.int32, (X, Y, Z), 1)
    iz = lax.broadcasted_iota(jnp.int32, (X, Y, Z), 2)
    ix = lax.broadcasted_iota(jnp.int32, (X, Y, Z), 0)
    red = ((ix + iy + iz) & 1) == 0
    wide = (X + 2, Y + 8, Z + 128)
    red_wide = (
        (
            lax.broadcasted_iota(jnp.int32, wide, 0)
            + lax.broadcasted_iota(jnp.int32, wide, 1)
            + lax.broadcasted_iota(jnp.int32, wide, 2)
        )
        & 1
    ) == 1

    def pack(tile, at):
        acc = jnp.broadcast_to(tile[0, :, at : at + 1], (Y, 128))
        for x in range(1, X):
            acc = jnp.where(lane == x, jnp.broadcast_to(tile[x, :, at : at + 1], (Y, 128)), acc)
        return acc

    def stage_layer(ch, p, k):
        sx[ch, 0] = p[k]
        sx[ch, 1] = p[X - 1 - k]
        sy[ch, 0] = p[:, k : k + 1, :]
        sy[ch, 1] = p[:, Y - 1 - k : Y - k, :]

        @pl.when(has[2][0])
        def _():
            sz[ch, 0] = pack(p[:, :, :128], k)

        @pl.when(has[2][1])
        def _():
            sz[ch, 1] = pack(p[:, :, Z - 128 :], 127 - k)

    def stage_black(ch, p):
        sx[ch, 0] = jnp.where(red[0], p[1], p[0])
        sx[ch, 1] = jnp.where(red[X - 1], p[X - 2], p[X - 1])
        low = p[:, :8]
        sy[ch, 0] = jnp.where(red[:, :8], pltpu.roll(low, 7, 1), low)[:, 0:1, :]
        high = p[:, Y - 8 :]
        sy[ch, 1] = jnp.where(red[:, Y - 8 :], pltpu.roll(high, 1, 1), high)[:, 7:8, :]

        @pl.when(has[2][0])
        def _():
            t = p[:, :, :128]
            sz[ch, 0] = pack(jnp.where(red[:, :, :128], pltpu.roll(t, 127, 2), t), 0)

        @pl.when(has[2][1])
        def _():
            t = p[:, :, Z - 128 :]
            sz[ch, 1] = pack(jnp.where(red[:, :, Z - 128 :], pltpu.roll(t, 1, 2), t), 127)

    def start(ch, parity, edge_parity):
        if edge_parity is not None:
            for e, a, b in edges:

                @pl.when(has_edge(e, a, b))
                def _():
                    edge_copy(ch, e, a, b, edge_parity).start()

        for d, side in faces:

            @pl.when(has[d][side])
            def _():
                face_copy(ch, d, side, parity).start()

    def finish(ch, parity, edge_parity):
        for d, side in faces:

            @pl.when(has[d][side])
            def _():
                face_copy(ch, d, side, parity, True).wait_recv()
                face_copy(ch, d, side, parity).wait_send()

        if edge_parity is not None:
            for e, a, b in edges:

                @pl.when(has_edge(e, a, b))
                def _():
                    edge_copy(ch, e, a, b, edge_parity, True).wait_recv()
                    edge_copy(ch, e, a, b, edge_parity).wait_send()

    def columns(packed, xs):
        return jnp.stack(
            [jnp.broadcast_to(packed[:, x : x + 1], (packed.shape[0], 128)) for x in xs], axis=0
        )

    near_y = sub_y < 4
    near_z = lane_z < 64

    def widen(p, ch, with_edges, second=None):
        y_plus = jnp.broadcast_to(hy[ch, 1], (X, 8, Z))
        y_minus = jnp.broadcast_to(hy[ch, 0], (X, 8, Z))
        z_plus = columns(hz[ch, 1], range(X))
        z_minus = columns(hz[ch, 0], range(X))
        if second is None:
            ytile = jnp.where(near_y, y_plus, y_minus)
            ztile = jnp.where(near_z, z_plus, z_minus)
        else:
            y_plus2 = jnp.broadcast_to(hy[second, 1], (X, 8, Z))
            y_minus2 = jnp.broadcast_to(hy[second, 0], (X, 8, Z))
            z_plus2 = columns(hz[second, 1], range(X))
            z_minus2 = columns(hz[second, 0], range(X))
            ytile = jnp.where(
                near_y,
                jnp.where(sub_y == 0, y_plus, y_plus2),
                jnp.where(sub_y == 7, y_minus, y_minus2),
            )
            ztile = jnp.where(
                near_z,
                jnp.where(lane_z == 0, z_plus, z_plus2),
                jnp.where(lane_z == 127, z_minus, z_minus2),
            )
        if with_edges:
            yz = []
            for side in range(2):
                rows8 = jnp.where(near_y[0, :, :128], hyz[ch, 1, side], hyz[ch, 0, side])
                yz.append(columns(rows8, range(X)))
            yztile = jnp.where(near_z[:, :8], yz[1], yz[0])
        else:
            yztile = jnp.zeros((X, 8, 128), jnp.float32)
        top = jnp.concatenate([p, ztile], axis=2)
        core = jnp.concatenate([top, jnp.concatenate([ytile, yztile], axis=2)], axis=1)
        planes = []
        for side in range(2):
            if with_edges:
                xy = jnp.where(
                    near_y[0],
                    jnp.broadcast_to(hxy[ch, side, 1], (8, Z)),
                    jnp.broadcast_to(hxy[ch, side, 0], (8, Z)),
                )
                at = 0 if side else X - 1
                xz = jnp.where(
                    near_z[0],
                    columns(hxz[ch, side, 1], (at,))[0],
                    columns(hxz[ch, side, 0], (at,))[0],
                )
            else:
                xy = jnp.zeros((8, Z), jnp.float32)
                xz = jnp.zeros((Y, 128), jnp.float32)
            first = jnp.concatenate([hx[ch, side], xz], axis=1)
            last = jnp.concatenate([xy, jnp.zeros((8, 128), jnp.float32)], axis=1)
            planes.append(jnp.concatenate([first, last], axis=0)[None])
        return jnp.concatenate([planes[0], core, planes[1]], axis=0)

    def around(v, lowest, highest):
        return (
            jnp.concatenate([v[1:], highest], axis=0),
            jnp.concatenate([lowest, v[:-1]], axis=0),
            pltpu.roll(v, Y + 7, 1),
            pltpu.roll(v, 1, 1),
            pltpu.roll(v, Z + 127, 2),
            pltpu.roll(v, 1, 2),
        )

    def wide_update(v):
        u = srd[...]
        for i, one in enumerate(around(v, v[:1], v[X + 1 :])):
            u = u + wts[i] * one
        return u

    def own(v):
        return v[1 : X + 1, :Y, :Z]

    def own_update(v):
        besides = (
            v[2:, :Y, :Z],
            v[:X, :Y, :Z],
            pltpu.roll(v[1 : X + 1, :, :Z], Y + 7, 1)[:, :Y],
            pltpu.roll(v[1 : X + 1, :, :Z], 1, 1)[:, :Y],
            pltpu.roll(v[1 : X + 1, :Y], Z + 127, 2)[:, :, :Z],
            pltpu.roll(v[1 : X + 1, :Y], 1, 2)[:, :, :Z],
        )
        u = srd[1 : X + 1, :Y, :Z]
        for i, one in enumerate(besides):
            u = u + wts[i, 1 : X + 1, :Y, :Z] * one
        return u

    def sweep(p, ch):
        v = widen(p, ch, True)
        v = jnp.where(red_wide, wide_update(v), v)
        return jnp.where(red, own(v), own_update(v))

    def gather_copy(buf, staged, which, off):
        return pltpu.make_async_remote_copy(
            src_ref=staged,
            dst_ref=buf.at[here[2]],
            send_sem=g_send.at[which, off - 1],
            recv_sem=g_recv.at[which, off - 1],
            device_id={"gz": lax.rem(here[2] + off, n_gz)},
            device_id_type=MESH,
        )

    def gather_start(buf, staged, which, value):
        staged[...] = value
        for off in range(1, n_gz):
            gather_copy(buf, staged, which, off).start()
        buf[here[2]] = value

    def gather_wait(buf, staged, which):
        for off in range(1, n_gz):
            gather_copy(buf, staged, which, off).wait_recv()
        return jnp.concatenate([buf[j] for j in range(n_gz)], axis=1)

    def pool(v):
        for h in range(2):
            part = v[:, :, 128 * h : 128 * h + 128].reshape(X // 2, 2, Y, 128)
            tmp[h] = (part[:, 0] + part[:, 1]).reshape(X // 2 * Y, 128)
        rows = X // 2 * Y // 2
        halves = [
            tmp[h, pl.ds(0, rows, stride=2), :] + tmp[h, pl.ds(1, rows, stride=2), :]
            for h in range(2)
        ]
        return exact_dot(jnp.concatenate(halves, axis=1), pool_m[...]) * 0.125

    loads[0].wait()
    loads[1].wait()
    c = con[...] * jnp.where(msk[...] > 0, clog_factor, 1.0)
    stage_layer(0, c, 0)
    stage_layer(1, c, 1)
    loads[2].wait()
    loads[3].wait()
    stage_layer(2, src[...], 0)
    pl.semaphore_wait(barrier, greeted)
    start(0, 0, 0)

    k_of = lax.broadcasted_iota(jnp.int32, (Z, ZC), 0)
    j_of = lax.broadcasted_iota(jnp.int32, (Z, ZC), 1)
    pool_m[...] = jnp.where((k_of >> 1) == j_of, 1.0, 0.0).astype(jnp.bfloat16)
    k_of = lax.broadcasted_iota(jnp.int32, (ZC, Z), 1)
    j_of = lax.broadcasted_iota(jnp.int32, (ZC, Z), 0)
    prol_m[...] = jnp.where((k_of >> 1) == j_of, 1.0, 0.0).astype(jnp.bfloat16)
    gather_start(cond_all, cond_send, 0, pool(c))

    rows = X // 2 * Y // 2
    col = lax.broadcasted_iota(jnp.int32, (rows, ids.shape[3]), 0)
    hit = jnp.zeros((rows, ids.shape[3]), jnp.float32)
    for o in range(ids.shape[2]):
        hit = jnp.maximum(hit, jnp.where(ids[0, 0, o : o + 1, :] == col, 1.0, 0.0))
    flag = jnp.max(hit, axis=1, keepdims=True)

    finish(0, 0, 0)
    cw = widen(c, 0, True, 1)
    pad = jnp.zeros((Y, 128), jnp.float32)
    second = [
        jnp.concatenate(
            [
                jnp.concatenate([hx[1, side], pad], axis=1),
                jnp.zeros((8, Z + 128), jnp.float32),
            ],
            axis=0,
        )[None]
        for side in range(2)
    ]
    w = [0.5 * (cw + one) for one in around(cw, second[0], second[1])]
    dg = shift_fine + w[0] + w[1] + w[2] + w[3] + w[4] + w[5]
    rd = jnp.where(cw > 0.0, 1.0 / dg, 0.0)
    diag[...] = own(dg)
    v = widen(src[...], 2, False) * rd
    srd[...] = v
    for i in range(6):
        wts[i] = w[i] * rd
    v = jnp.where(red_wide, v, 0.0)
    p = jnp.where(red, own(v), own_update(v))
    stage_black(3, p)
    start(3, 1, 1)

    def factor(state, stage):
        lower, main, upper = state
        stride = 1 << stage
        rm = 1.0 / main
        low = -lower * pltpu.roll(rm, stride, 1)
        high = -upper * pltpu.roll(rm, length - stride, 1)
        fac[2 * stage] = low
        fac[2 * stage + 1] = high
        main = (
            main + low * pltpu.roll(upper, stride, 1) + high * pltpu.roll(lower, length - stride, 1)
        )
        lower = low * pltpu.roll(lower, stride, 1)
        upper = high * pltpu.roll(upper, length - stride, 1)
        return lower, main, upper

    cond = gather_wait(cond_all, cond_send, 0)
    at = lax.broadcasted_iota(jnp.int32, cond.shape, 1)
    before = cond + pltpu.roll(cond, 1, 1)
    after = cond + pltpu.roll(cond, length - 1, 1)
    left_sum = jnp.where(at == 0, cond, before)
    right_sum = jnp.where(at == length - 1, cond, after)
    state = (
        jnp.where(at == 0, 0.0, -before),
        1.0 / (CZ * CZ) + left_sum + right_sum,
        jnp.where(at == length - 1, 0.0, -after),
    )
    per = stages // 2
    for stage in range(0, per):
        state = factor(state, stage)
    finish(3, 1, 1)
    p = sweep(p, 3)
    stage_black(4, p)
    start(4, 0, None)
    for stage in range(per, stages):
        state = factor(state, stage)
    fac[2 * stages] = (2.0 / (CZ * CZ)) / state[1]
    finish(4, 0, None)
    u = own_update(widen(p, 4, False))
    rhs = pool(jnp.where(red, diag[...] * (u - p), 0.0)) * flag
    gather_start(rhs_all, rhs_send, 1, rhs)
    values = gather_wait(rhs_all, rhs_send, 1)
    for stage in range(stages):
        stride = 1 << stage
        values = (
            values
            + fac[2 * stage] * pltpu.roll(values, stride, 1)
            + fac[2 * stage + 1] * pltpu.roll(values, length - stride, 1)
        )
    rhs_all[...] = jnp.stack(
        [
            (values * fac[2 * stages])[:, ZC * j : ZC * j + ZC]
            for j in range(n_gz)
        ],
        axis=0,
    )
    mine = rhs_all[here[2]]
    fine = exact_dot(mine, prol_m[...])
    for h in range(2):
        part = fine[:, 128 * h : 128 * h + 128]
        tmp[h, pl.ds(0, rows, stride=2), :] = part
        tmp[h, pl.ds(1, rows, stride=2), :] = part
    add = jnp.concatenate([tmp[0], tmp[1]], axis=1).reshape(X // 2, 1, Y, Z)
    p = p + jnp.broadcast_to(add, (X // 2, 2, Y, Z)).reshape(X, Y, Z)

    stage_black(5, p)
    start(5, 1, 0)
    finish(5, 1, 0)
    p = sweep(p, 5)
    stage_black(6, p)
    start(6, 0, 1)
    finish(6, 0, 1)
    out_ref[...] = sweep(p, 6)

    for off in range(1, n_gz):
        gather_copy(cond_all, cond_send, 0, off).wait_send()
        gather_copy(rhs_all, rhs_send, 1, off).wait_send()


def shards(sizes, source, conduct, solid_mask, line_ids):
    X, Y, Z = source.shape
    ZC = Z // 2
    rows = X // 2 * Y // 2
    n_gz = sizes[2]
    length = n_gz * ZC
    stages = (length - 1).bit_length()
    f32 = jnp.float32
    V = pltpu.VMEM
    dma = pltpu.SemaphoreType.DMA
    return pl.pallas_call(
        functools.partial(kernel, sizes),
        out_shape=jax.ShapeDtypeStruct((X, Y, Z), f32),
        in_specs=[pl.BlockSpec(memory_space=pltpu.HBM)] * 4,
        out_specs=pl.BlockSpec(memory_space=pltpu.VMEM),
        scratch_shapes=[
            V((X, Y, Z), f32),
            V((X, Y, Z), f32),
            V((X, Y, Z), jnp.int32),
            V(line_ids.shape, jnp.int32),
            V((CHANNELS, 2, Y, Z), f32),
            V((CHANNELS, 2, X, 1, Z), f32),
            V((CHANNELS, 2, Y, 128), f32),
            V((CHANNELS, 2, Y, Z), f32),
            V((CHANNELS, 2, X, 1, Z), f32),
            V((CHANNELS, 2, Y, 128), f32),
            V((CHANNELS, 2, 2, 1, Z), f32),
            V((CHANNELS, 2, 2, Y, 128), f32),
            V((CHANNELS, 2, 2, 8, 128), f32),
            V((6, X + 2, Y + 8, Z + 128), f32),
            V((X, Y, Z), f32),
            V((X + 2, Y + 8, Z + 128), f32),
            V((2, X // 2 * Y, 128), f32),
            V((Z, ZC), jnp.bfloat16),
            V((ZC, Z), jnp.bfloat16),
            V((n_gz, rows, ZC), f32),
            V((n_gz, rows, ZC), f32),
            V((rows, ZC), f32),
            V((rows, ZC), f32),
            V((2 * stages + 1, rows, length), f32),
            dma((4,)),
            dma((18,)),
            dma((2, 18)),
            dma((2, n_gz - 1)),
            dma((2, n_gz - 1)),
        ],
        compiler_params=pltpu.CompilerParams(
            collective_id=0, has_side_effects=True, vmem_limit_bytes=67043328
        ),
        name="cycle",
    )(source, conduct, solid_mask, line_ids)


def solution(mesh):
    sizes = tuple(mesh.shape[a] for a in AXES)
    in_specs = (
        P("gx", "gy", "gz"),
        P("gx", "gy", "gz"),
        P("gx", "gy", "gz"),
        P("gx", "gy", None, None),
    )
    out_specs = P("gx", "gy", "gz")
    return jax.shard_map(
        functools.partial(shards, sizes),
        mesh=mesh,
        in_specs=in_specs,
        out_specs=out_specs,
        check_vma=False,
    )
```

```python
import functools

import jax
import jax.numpy as jnp
from jax import lax
from jax.experimental import pallas as pl
from jax.experimental.pallas import tpu as pltpu
from jax.sharding import PartitionSpec as P

CZ = 256
CHANNELS = 7
EDGES = ((0, 1), (0, 2), (1, 2))
clog_factor = 0.2
shift_fine = 0.001
MESH = pl.DeviceIdType.MESH
AXES = ("gx", "gy", "gz")


def split3(x):
    hi = x.astype(jnp.bfloat16)
    rest = x - hi.astype(jnp.float32)
    mid = rest.astype(jnp.bfloat16)
    low = (rest - mid.astype(jnp.float32)).astype(jnp.bfloat16)
    return jnp.concatenate([hi, mid, low], axis=0)


def exact_dot(x, ones):
    rows = x.shape[0]
    y = jnp.dot(split3(x), ones, preferred_element_type=jnp.float32)
    return (y[2 * rows :] + y[rows : 2 * rows]) + y[:rows]


def kernel(
    sizes,
    src_hbm,
    con_hbm,
    msk_hbm,
    ids_hbm,
    out_ref,
    src,
    con,
    msk,
    ids,
    hx,
    hy,
    hz,
    sx,
    sy,
    sz,
    hxy,
    hxz,
    hyz,
    wts,
    field,
    after,
    diag,
    srd,
    tmp,
    pool_m,
    prol_m,
    cond_all,
    rhs_all,
    cond_send,
    rhs_send,
    fac,
    in_sem,
    send_sem,
    recv_sem,
    g_send,
    g_recv,
):
    X, Y, Z = src.shape
    ZC = Z // 2
    here = [lax.axis_index(a) for a in AXES]
    n_gz = sizes[2]
    length = n_gz * ZC
    stages = (length - 1).bit_length()

    loads = [
        pltpu.make_async_copy(a, b, in_sem.at[i])
        for i, (a, b) in enumerate(
            ((con_hbm, con), (msk_hbm, msk), (src_hbm, src), (ids_hbm, ids))
        )
    ]
    for load in loads:
        load.start()

    halo = (hx, hy, hz)
    outgoing = (sx, sy, sz)
    edge_halo = (hxy, hxz, hyz)
    has = [(here[d] > 0, here[d] < sizes[d] - 1) for d in range(3)]

    def beside(d, side):
        return {AXES[d]: here[d] + (2 * side - 1)}

    faces = [(d, side) for d in (2, 0, 1) for side in range(2)]
    edges = [(e, a, b) for e in range(3) for a in range(2) for b in range(2)]

    def has_edge(e, a, b):
        return jnp.logical_and(has[EDGES[e][0]][a], has[EDGES[e][1]][b])

    for d, side in faces:

        @pl.when(jnp.logical_not(has[d][side]))
        def _():
            for r in range(CHANNELS):
                halo[d][r, side] = jnp.zeros(halo[d].shape[2:], jnp.float32)

    for e, a, b in edges:

        @pl.when(jnp.logical_not(has_edge(e, a, b)))
        def _():
            for r in (0, 3, 5, 6):
                edge_halo[e][r, a, b] = jnp.zeros(edge_halo[e].shape[3:], jnp.float32)

    barrier = pltpu.get_barrier_semaphore()
    greeted = n_gz - 1
    for d, side in faces:
        if d == 2:
            continue
        greeted = greeted + has[d][side].astype(jnp.int32)

        @pl.when(has[d][side])
        def _():
            pl.semaphore_signal(
                barrier, inc=1, device_id=beside(d, side), device_id_type=MESH
            )

    for e, a, b in edges:
        greeted = greeted + has_edge(e, a, b).astype(jnp.int32)

        @pl.when(has_edge(e, a, b))
        def _():
            pl.semaphore_signal(
                barrier,
                inc=1,
                device_id={**beside(EDGES[e][0], a), **beside(EDGES[e][1], b)},
                device_id_type=MESH,
            )

    for off in range(1, n_gz):
        pl.semaphore_signal(
            barrier,
            inc=1,
            device_id={"gz": lax.rem(here[2] + off, n_gz)},
            device_id_type=MESH,
        )

    def channels_of(ch):
        return pl.ds(0, 3) if ch == 0 else ch

    def face_copy(ch, d, side, parity, arrival=False):
        at = side if arrival else 1 - side
        return pltpu.make_async_remote_copy(
            src_ref=outgoing[d].at[channels_of(ch), side],
            dst_ref=halo[d].at[channels_of(ch), at],
            send_sem=send_sem.at[2 * d + side],
            recv_sem=recv_sem.at[parity, 2 * d + at],
            device_id=beside(d, side),
            device_id_type=MESH,
        )

    def edge_copy(ch, e, a, b, parity, arrival=False):
        to = (a, b) if arrival else (1 - a, 1 - b)
        if e == 0:
            piece = sy.at[ch, b, a * (X - 1)]
        elif e == 1:
            piece = sz.at[ch, b]
        else:
            piece = sz.at[ch, b, pl.ds(a * (Y - 8), 8)]
        return pltpu.make_async_remote_copy(
            src_ref=piece,
            dst_ref=edge_halo[e].at[ch, to[0], to[1]],
            send_sem=send_sem.at[6 + 4 * e + 2 * a + b],
            recv_sem=recv_sem.at[parity, 6 + 4 * e + 2 * to[0] + to[1]],
            device_id={**beside(EDGES[e][0], a), **beside(EDGES[e][1], b)},
            device_id_type=MESH,
        )

    lane = lax.broadcasted_iota(jnp.int32, (Y, 128), 1)
    sub_y = lax.broadcasted_iota(jnp.int32, (X, 8, Z), 1)
    lane_z = lax.broadcasted_iota(jnp.int32, (X, Y, 128), 2)
    iy = lax.broadcasted_iota(jnp.int32, (X, Y, Z), 1)
    iz = lax.broadcasted_iota(jnp.int32, (X, Y, Z), 2)
    ix = lax.broadcasted_iota(jnp.int32, (X, Y, Z), 0)
    red = ((ix + iy + iz) & 1) == 0
    wide = (X + 2, Y + 8, Z + 128)
    def pack(tile, at):
        acc = jnp.broadcast_to(tile[0, :, at : at + 1], (Y, 128))
        for x in range(1, X):
            acc = jnp.where(lane == x, jnp.broadcast_to(tile[x, :, at : at + 1], (Y, 128)), acc)
        return acc

    def stage_layer(ch, p, k):
        sx[ch, 0] = p[k]
        sx[ch, 1] = p[X - 1 - k]
        sy[ch, 0] = p[:, k : k + 1, :]
        sy[ch, 1] = p[:, Y - 1 - k : Y - k, :]

        @pl.when(has[2][0])
        def _():
            sz[ch, 0] = pack(p[:, :, :128], k)

        @pl.when(has[2][1])
        def _():
            sz[ch, 1] = pack(p[:, :, Z - 128 :], 127 - k)

    def stage_black(ch, p):
        sx[ch, 0] = jnp.where(red[0], p[1], p[0])
        sx[ch, 1] = jnp.where(red[X - 1], p[X - 2], p[X - 1])
        low = p[:, :8]
        sy[ch, 0] = jnp.where(red[:, :8], pltpu.roll(low, 7, 1), low)[:, 0:1, :]
        high = p[:, Y - 8 :]
        sy[ch, 1] = jnp.where(red[:, Y - 8 :], pltpu.roll(high, 1, 1), high)[:, 7:8, :]

        @pl.when(has[2][0])
        def _():
            t = p[:, :, :128]
            sz[ch, 0] = pack(jnp.where(red[:, :, :128], pltpu.roll(t, 127, 2), t), 0)

        @pl.when(has[2][1])
        def _():
            t = p[:, :, Z - 128 :]
            sz[ch, 1] = pack(jnp.where(red[:, :, Z - 128 :], pltpu.roll(t, 1, 2), t), 127)

    def start(ch, parity, edge_parity):
        if edge_parity is not None:
            for e, a, b in edges:

                @pl.when(has_edge(e, a, b))
                def _():
                    edge_copy(ch, e, a, b, edge_parity).start()

        for d, side in faces:

            @pl.when(has[d][side])
            def _():
                face_copy(ch, d, side, parity).start()

    def finish(ch, parity, edge_parity):
        for d, side in faces:

            @pl.when(has[d][side])
            def _():
                face_copy(ch, d, side, parity, True).wait_recv()
                face_copy(ch, d, side, parity).wait_send()

        if edge_parity is not None:
            for e, a, b in edges:

                @pl.when(has_edge(e, a, b))
                def _():
                    edge_copy(ch, e, a, b, edge_parity, True).wait_recv()
                    edge_copy(ch, e, a, b, edge_parity).wait_send()

    def columns(packed, xs):
        return jnp.stack(
            [jnp.broadcast_to(packed[:, x : x + 1], (packed.shape[0], 128)) for x in xs], axis=0
        )

    near_y = sub_y < 4
    near_z = lane_z < 64

    def widen(p, ch, with_edges, second=None):
        y_plus = jnp.broadcast_to(hy[ch, 1], (X, 8, Z))
        y_minus = jnp.broadcast_to(hy[ch, 0], (X, 8, Z))
        z_plus = columns(hz[ch, 1], range(X))
        z_minus = columns(hz[ch, 0], range(X))
        if second is None:
            ytile = jnp.where(near_y, y_plus, y_minus)
            ztile = jnp.where(near_z, z_plus, z_minus)
        else:
            y_plus2 = jnp.broadcast_to(hy[second, 1], (X, 8, Z))
            y_minus2 = jnp.broadcast_to(hy[second, 0], (X, 8, Z))
            z_plus2 = columns(hz[second, 1], range(X))
            z_minus2 = columns(hz[second, 0], range(X))
            ytile = jnp.where(
                near_y,
                jnp.where(sub_y == 0, y_plus, y_plus2),
                jnp.where(sub_y == 7, y_minus, y_minus2),
            )
            ztile = jnp.where(
                near_z,
                jnp.where(lane_z == 0, z_plus, z_plus2),
                jnp.where(lane_z == 127, z_minus, z_minus2),
            )
        if with_edges:
            yz = []
            for side in range(2):
                rows8 = jnp.where(near_y[0, :, :128], hyz[ch, 1, side], hyz[ch, 0, side])
                yz.append(columns(rows8, range(X)))
            yztile = jnp.where(near_z[:, :8], yz[1], yz[0])
        else:
            yztile = jnp.zeros((X, 8, 128), jnp.float32)
        top = jnp.concatenate([p, ztile], axis=2)
        core = jnp.concatenate([top, jnp.concatenate([ytile, yztile], axis=2)], axis=1)
        planes = []
        for side in range(2):
            if with_edges:
                xy = jnp.where(
                    near_y[0],
                    jnp.broadcast_to(hxy[ch, side, 1], (8, Z)),
                    jnp.broadcast_to(hxy[ch, side, 0], (8, Z)),
                )
                at = 0 if side else X - 1
                xz = jnp.where(
                    near_z[0],
                    columns(hxz[ch, side, 1], (at,))[0],
                    columns(hxz[ch, side, 0], (at,))[0],
                )
            else:
                xy = jnp.zeros((8, Z), jnp.float32)
                xz = jnp.zeros((Y, 128), jnp.float32)
            first = jnp.concatenate([hx[ch, side], xz], axis=1)
            last = jnp.concatenate([xy, jnp.zeros((8, 128), jnp.float32)], axis=1)
            planes.append(jnp.concatenate([first, last], axis=0)[None])
        return jnp.concatenate([planes[0], core, planes[1]], axis=0)

    line_of = lax.broadcasted_iota(jnp.int32, wide[1:], 0)
    cell_of = lax.broadcasted_iota(jnp.int32, wide[1:], 1)
    odd = ((line_of + cell_of) & 1) == 1
    reds = (odd, jnp.logical_not(odd))

    def around(v, low, high):
        return (
            high,
            low,
            pltpu.roll(v, Y + 7, 0),
            pltpu.roll(v, 1, 0),
            pltpu.roll(v, Z + 127, 1),
            pltpu.roll(v, 1, 1),
        )

    def own_plane(field, i):
        besides = (
            field[min(i + 1, X + 1), :Y, :Z],
            field[max(i - 1, 0), :Y, :Z],
            pltpu.roll(field[i, :, :Z], Y + 7, 0)[:Y],
            pltpu.roll(field[i, :, :Z], 1, 0)[:Y],
            pltpu.roll(field[i, :Y, :], Z + 127, 1)[:, :Z],
            pltpu.roll(field[i, :Y, :], 1, 1)[:, :Z],
        )
        u = srd[i, :Y, :Z]
        for k, one in enumerate(besides):
            u = u + wts[k, i, :Y, :Z] * one
        return u

    def black_update():
        return jnp.stack(
            [
                jnp.where(reds[i % 2][:Y, :Z], after[i, :Y, :Z], own_plane(after, i))
                for i in range(1, X + 1)
            ],
            axis=0,
        )

    def sweep(p, ch):
        field[...] = widen(p, ch, True)
        for i in range(X + 2):
            mask = reds[i % 2]
            if i in (0, X + 1):
                after[i, :Y, :Z] = jnp.where(
                    mask[:Y, :Z], own_plane(field, i), field[i, :Y, :Z]
                )
            else:
                v = field[i]
                u = srd[i]
                for k, one in enumerate(around(v, field[i - 1], field[i + 1])):
                    u = u + wts[k, i] * one
                after[i] = jnp.where(mask, u, v)
        return black_update()

    def gather_copy(buf, staged, which, off):
        return pltpu.make_async_remote_copy(
            src_ref=staged,
            dst_ref=buf.at[here[2]],
            send_sem=g_send.at[which, off - 1],
            recv_sem=g_recv.at[which, off - 1],
            device_id={"gz": lax.rem(here[2] + off, n_gz)},
            device_id_type=MESH,
        )

    def gather_start(buf, staged, which, value):
        staged[...] = value
        for off in range(1, n_gz):
            gather_copy(buf, staged, which, off).start()
        buf[here[2]] = value

    def gather_wait(buf, staged, which):
        for off in range(1, n_gz):
            gather_copy(buf, staged, which, off).wait_recv()
        return jnp.concatenate([buf[j] for j in range(n_gz)], axis=1)

    def pool(v):
        for h in range(2):
            part = v[:, :, 128 * h : 128 * h + 128].reshape(X // 2, 2, Y, 128)
            tmp[h] = (part[:, 0] + part[:, 1]).reshape(X // 2 * Y, 128)
        rows = X // 2 * Y // 2
        halves = [
            tmp[h, pl.ds(0, rows, stride=2), :] + tmp[h, pl.ds(1, rows, stride=2), :]
            for h in range(2)
        ]
        return exact_dot(jnp.concatenate(halves, axis=1), pool_m[...]) * 0.125

    loads[0].wait()
    loads[1].wait()
    c = con[...] * jnp.where(msk[...] > 0, clog_factor, 1.0)
    stage_layer(0, c, 0)
    stage_layer(1, c, 1)
    loads[2].wait()
    loads[3].wait()
    stage_layer(2, src[...], 0)
    pl.semaphore_wait(barrier, greeted)
    start(0, 0, 0)

    k_of = lax.broadcasted_iota(jnp.int32, (Z, ZC), 0)
    j_of = lax.broadcasted_iota(jnp.int32, (Z, ZC), 1)
    pool_m[...] = jnp.where((k_of >> 1) == j_of, 1.0, 0.0).astype(jnp.bfloat16)
    k_of = lax.broadcasted_iota(jnp.int32, (ZC, Z), 1)
    j_of = lax.broadcasted_iota(jnp.int32, (ZC, Z), 0)
    prol_m[...] = jnp.where((k_of >> 1) == j_of, 1.0, 0.0).astype(jnp.bfloat16)
    gather_start(cond_all, cond_send, 0, pool(c))

    rows = X // 2 * Y // 2
    col = lax.broadcasted_iota(jnp.int32, (rows, ids.shape[3]), 0)
    hit = jnp.zeros((rows, ids.shape[3]), jnp.float32)
    for o in range(ids.shape[2]):
        hit = jnp.maximum(hit, jnp.where(ids[0, 0, o : o + 1, :] == col, 1.0, 0.0))
    flag = jnp.max(hit, axis=1, keepdims=True)

    finish(0, 0, 0)
    field[...] = widen(c, 0, True, 1)
    after[...] = widen(src[...], 2, False)
    second = [
        jnp.concatenate(
            [
                jnp.concatenate([hx[1, side], jnp.zeros((Y, 128), jnp.float32)], axis=1),
                jnp.zeros((8, Z + 128), jnp.float32),
            ],
            axis=0,
        )
        for side in range(2)
    ]
    for i in range(X + 2):
        v = field[i]
        low = field[i - 1] if i else second[0]
        high = field[i + 1] if i < X + 1 else second[1]
        w = [0.5 * (v + one) for one in around(v, low, high)]
        dg = shift_fine + w[0] + w[1] + w[2] + w[3] + w[4] + w[5]
        rd = jnp.where(v > 0.0, 1.0 / dg, 0.0)
        if 0 < i < X + 1:
            diag[i - 1] = dg[:Y, :Z]
        for k in range(6):
            wts[k, i] = w[k] * rd
        v = after[i] * rd
        srd[i] = v
        after[i] = jnp.where(reds[i % 2], v, 0.0)
    p = black_update()
    stage_black(3, p)
    start(3, 1, 1)

    def factor(state, stage):
        lower, main, upper = state
        stride = 1 << stage
        rm = 1.0 / main
        low = -lower * pltpu.roll(rm, stride, 1)
        high = -upper * pltpu.roll(rm, length - stride, 1)
        fac[2 * stage] = low
        fac[2 * stage + 1] = high
        main = (
            main + low * pltpu.roll(upper, stride, 1) + high * pltpu.roll(lower, length - stride, 1)
        )
        lower = low * pltpu.roll(lower, stride, 1)
        upper = high * pltpu.roll(upper, length - stride, 1)
        return lower, main, upper

    cond = gather_wait(cond_all, cond_send, 0)
    at = lax.broadcasted_iota(jnp.int32, cond.shape, 1)
    sum_low = cond + pltpu.roll(cond, 1, 1)
    sum_high = cond + pltpu.roll(cond, length - 1, 1)
    left_sum = jnp.where(at == 0, cond, sum_low)
    right_sum = jnp.where(at == length - 1, cond, sum_high)
    state = (
        jnp.where(at == 0, 0.0, -sum_low),
        1.0 / (CZ * CZ) + left_sum + right_sum,
        jnp.where(at == length - 1, 0.0, -sum_high),
    )
    per = stages // 2
    for stage in range(0, per):
        state = factor(state, stage)
    finish(3, 1, 1)
    p = sweep(p, 3)
    stage_black(4, p)
    start(4, 0, None)
    for stage in range(per, stages):
        state = factor(state, stage)
    fac[2 * stages] = (2.0 / (CZ * CZ)) / state[1]
    finish(4, 0, None)
    after[...] = widen(p, 4, False)
    residual = jnp.stack(
        [
            jnp.where(
                reds[i % 2][:Y, :Z],
                diag[i - 1] * (own_plane(after, i) - after[i, :Y, :Z]),
                0.0,
            )
            for i in range(1, X + 1)
        ],
        axis=0,
    )
    rhs = pool(residual) * flag
    gather_start(rhs_all, rhs_send, 1, rhs)
    values = gather_wait(rhs_all, rhs_send, 1)
    for stage in range(stages):
        stride = 1 << stage
        values = (
            values
            + fac[2 * stage] * pltpu.roll(values, stride, 1)
            + fac[2 * stage + 1] * pltpu.roll(values, length - stride, 1)
        )
    rhs_all[...] = jnp.stack(
        [
            (values * fac[2 * stages])[:, ZC * j : ZC * j + ZC]
            for j in range(n_gz)
        ],
        axis=0,
    )
    mine = rhs_all[here[2]]
    fine = exact_dot(mine, prol_m[...])
    for h in range(2):
        part = fine[:, 128 * h : 128 * h + 128]
        tmp[h, pl.ds(0, rows, stride=2), :] = part
        tmp[h, pl.ds(1, rows, stride=2), :] = part
    add = jnp.concatenate([tmp[0], tmp[1]], axis=1).reshape(X // 2, 1, Y, Z)
    p = p + jnp.broadcast_to(add, (X // 2, 2, Y, Z)).reshape(X, Y, Z)

    stage_black(5, p)
    start(5, 1, 0)
    finish(5, 1, 0)
    p = sweep(p, 5)
    stage_black(6, p)
    start(6, 0, 1)
    finish(6, 0, 1)
    out_ref[...] = sweep(p, 6)

    for off in range(1, n_gz):
        gather_copy(cond_all, cond_send, 0, off).wait_send()
        gather_copy(rhs_all, rhs_send, 1, off).wait_send()


def shards(sizes, source, conduct, solid_mask, line_ids):
    X, Y, Z = source.shape
    ZC = Z // 2
    rows = X // 2 * Y // 2
    n_gz = sizes[2]
    length = n_gz * ZC
    stages = (length - 1).bit_length()
    f32 = jnp.float32
    V = pltpu.VMEM
    dma = pltpu.SemaphoreType.DMA
    return pl.pallas_call(
        functools.partial(kernel, sizes),
        out_shape=jax.ShapeDtypeStruct((X, Y, Z), f32),
        in_specs=[pl.BlockSpec(memory_space=pltpu.HBM)] * 4,
        out_specs=pl.BlockSpec(memory_space=pltpu.VMEM),
        scratch_shapes=[
            V((X, Y, Z), f32),
            V((X, Y, Z), f32),
            V((X, Y, Z), jnp.int32),
            V(line_ids.shape, jnp.int32),
            V((CHANNELS, 2, Y, Z), f32),
            V((CHANNELS, 2, X, 1, Z), f32),
            V((CHANNELS, 2, Y, 128), f32),
            V((CHANNELS, 2, Y, Z), f32),
            V((CHANNELS, 2, X, 1, Z), f32),
            V((CHANNELS, 2, Y, 128), f32),
            V((CHANNELS, 2, 2, 1, Z), f32),
            V((CHANNELS, 2, 2, Y, 128), f32),
            V((CHANNELS, 2, 2, 8, 128), f32),
            V((6, X + 2, Y + 8, Z + 128), f32),
            V((X + 2, Y + 8, Z + 128), f32),
            V((X + 2, Y + 8, Z + 128), f32),
            V((X, Y, Z), f32),
            V((X + 2, Y + 8, Z + 128), f32),
            V((2, X // 2 * Y, 128), f32),
            V((Z, ZC), jnp.bfloat16),
            V((ZC, Z), jnp.bfloat16),
            V((n_gz, rows, ZC), f32),
            V((n_gz, rows, ZC), f32),
            V((rows, ZC), f32),
            V((rows, ZC), f32),
            V((2 * stages + 1, rows, length), f32),
            dma((4,)),
            dma((18,)),
            dma((2, 18)),
            dma((2, n_gz - 1)),
            dma((2, n_gz - 1)),
        ],
        compiler_params=pltpu.CompilerParams(
            collective_id=0, has_side_effects=True, vmem_limit_bytes=67043328
        ),
        name="cycle",
    )(source, conduct, solid_mask, line_ids)


def solution(mesh):
    sizes = tuple(mesh.shape[a] for a in AXES)
    in_specs = (
        P("gx", "gy", "gz"),
        P("gx", "gy", "gz"),
        P("gx", "gy", "gz"),
        P("gx", "gy", None, None),
    )
    out_specs = P("gx", "gy", "gz")
    return jax.shard_map(
        functools.partial(shards, sizes),
        mesh=mesh,
        in_specs=in_specs,
        out_specs=out_specs,
        check_vma=False,
    )
```

```python
import functools

import jax
import jax.numpy as jnp
from jax import lax
from jax.experimental import pallas as pl
from jax.experimental.pallas import tpu as pltpu
from jax.sharding import PartitionSpec as P

CZ = 256
CHANNELS = 7
EDGES = ((0, 1), (0, 2), (1, 2))
clog_factor = 0.2
shift_fine = 0.001
MESH = pl.DeviceIdType.MESH
AXES = ("gx", "gy", "gz")


def split3(x):
    hi = x.astype(jnp.bfloat16)
    rest = x - hi.astype(jnp.float32)
    mid = rest.astype(jnp.bfloat16)
    low = (rest - mid.astype(jnp.float32)).astype(jnp.bfloat16)
    return jnp.concatenate([hi, mid, low], axis=0)


def exact_dot(x, ones):
    rows = x.shape[0]
    y = jnp.dot(split3(x), ones, preferred_element_type=jnp.float32)
    return (y[2 * rows :] + y[rows : 2 * rows]) + y[:rows]


def kernel(
    sizes,
    src_hbm,
    con_hbm,
    msk_hbm,
    ids_hbm,
    out_ref,
    src,
    con,
    msk,
    ids,
    hx,
    hy,
    hz,
    sx,
    sy,
    sz,
    hxy,
    hxz,
    hyz,
    wts,
    field,
    after,
    diag,
    srd,
    tmp,
    pool_m,
    prol_m,
    cond_all,
    rhs_all,
    cond_send,
    rhs_send,
    fac,
    in_sem,
    send_sem,
    recv_sem,
    g_send,
    g_recv,
):
    X, Y, Z = src.shape
    ZC = Z // 2
    here = [lax.axis_index(a) for a in AXES]
    n_gz = sizes[2]
    length = n_gz * ZC
    stages = (length - 1).bit_length()

    loads = [
        pltpu.make_async_copy(a, b, in_sem.at[i])
        for i, (a, b) in enumerate(
            ((con_hbm, con), (msk_hbm, msk), (src_hbm, src), (ids_hbm, ids))
        )
    ]
    for load in loads:
        load.start()

    halo = (hx, hy, hz)
    outgoing = (sx, sy, sz)
    edge_halo = (hxy, hxz, hyz)
    has = [(here[d] > 0, here[d] < sizes[d] - 1) for d in range(3)]

    def beside(d, side):
        return {AXES[d]: here[d] + (2 * side - 1)}

    faces = [(d, side) for d in (2, 0, 1) for side in range(2)]
    edges = [(e, a, b) for e in range(3) for a in range(2) for b in range(2)]

    def has_edge(e, a, b):
        return jnp.logical_and(has[EDGES[e][0]][a], has[EDGES[e][1]][b])

    for d, side in faces:

        @pl.when(jnp.logical_not(has[d][side]))
        def _():
            for r in range(CHANNELS):
                halo[d][r, side] = jnp.zeros(halo[d].shape[2:], jnp.float32)

    for e, a, b in edges:

        @pl.when(jnp.logical_not(has_edge(e, a, b)))
        def _():
            for r in (0, 3, 5, 6):
                edge_halo[e][r, a, b] = jnp.zeros(edge_halo[e].shape[3:], jnp.float32)

    barrier = pltpu.get_barrier_semaphore()
    greeted = n_gz - 1
    for d, side in faces:
        if d == 2:
            continue
        greeted = greeted + has[d][side].astype(jnp.int32)

        @pl.when(has[d][side])
        def _():
            pl.semaphore_signal(
                barrier, inc=1, device_id=beside(d, side), device_id_type=MESH
            )

    for e, a, b in edges:
        greeted = greeted + has_edge(e, a, b).astype(jnp.int32)

        @pl.when(has_edge(e, a, b))
        def _():
            pl.semaphore_signal(
                barrier,
                inc=1,
                device_id={**beside(EDGES[e][0], a), **beside(EDGES[e][1], b)},
                device_id_type=MESH,
            )

    for off in range(1, n_gz):
        pl.semaphore_signal(
            barrier,
            inc=1,
            device_id={"gz": lax.rem(here[2] + off, n_gz)},
            device_id_type=MESH,
        )

    def channels_of(ch):
        return pl.ds(0, 3) if ch == 0 else ch

    def face_copy(ch, d, side, parity, arrival=False):
        at = side if arrival else 1 - side
        return pltpu.make_async_remote_copy(
            src_ref=outgoing[d].at[channels_of(ch), side],
            dst_ref=halo[d].at[channels_of(ch), at],
            send_sem=send_sem.at[2 * d + side],
            recv_sem=recv_sem.at[parity, 2 * d + at],
            device_id=beside(d, side),
            device_id_type=MESH,
        )

    def edge_copy(ch, e, a, b, parity, arrival=False):
        to = (a, b) if arrival else (1 - a, 1 - b)
        if e == 0:
            piece = sy.at[ch, b, a * (X - 1)]
        elif e == 1:
            piece = sz.at[ch, b]
        else:
            piece = sz.at[ch, b, pl.ds(a * (Y - 8), 8)]
        return pltpu.make_async_remote_copy(
            src_ref=piece,
            dst_ref=edge_halo[e].at[ch, to[0], to[1]],
            send_sem=send_sem.at[6 + 4 * e + 2 * a + b],
            recv_sem=recv_sem.at[parity, 6 + 4 * e + 2 * to[0] + to[1]],
            device_id={**beside(EDGES[e][0], a), **beside(EDGES[e][1], b)},
            device_id_type=MESH,
        )

    lane = lax.broadcasted_iota(jnp.int32, (Y, 128), 1)
    sub_y = lax.broadcasted_iota(jnp.int32, (X, 8, Z), 1)
    lane_z = lax.broadcasted_iota(jnp.int32, (X, Y, 128), 2)
    iy = lax.broadcasted_iota(jnp.int32, (X, Y, Z), 1)
    iz = lax.broadcasted_iota(jnp.int32, (X, Y, Z), 2)
    ix = lax.broadcasted_iota(jnp.int32, (X, Y, Z), 0)
    red = ((ix + iy + iz) & 1) == 0
    wide = (X + 2, Y + 8, Z + 128)
    def pack(tile, at):
        acc = jnp.broadcast_to(tile[0, :, at : at + 1], (Y, 128))
        for x in range(1, X):
            acc = jnp.where(lane == x, jnp.broadcast_to(tile[x, :, at : at + 1], (Y, 128)), acc)
        return acc

    def stage_layer(ch, p, k):
        sx[ch, 0] = p[k]
        sx[ch, 1] = p[X - 1 - k]
        sy[ch, 0] = p[:, k : k + 1, :]
        sy[ch, 1] = p[:, Y - 1 - k : Y - k, :]

        @pl.when(has[2][0])
        def _():
            sz[ch, 0] = pack(p[:, :, :128], k)

        @pl.when(has[2][1])
        def _():
            sz[ch, 1] = pack(p[:, :, Z - 128 :], 127 - k)

    def stage_black(ch, p):
        sx[ch, 0] = jnp.where(red[0], p[1], p[0])
        sx[ch, 1] = jnp.where(red[X - 1], p[X - 2], p[X - 1])
        low = p[:, :8]
        sy[ch, 0] = jnp.where(red[:, :8], pltpu.roll(low, 7, 1), low)[:, 0:1, :]
        high = p[:, Y - 8 :]
        sy[ch, 1] = jnp.where(red[:, Y - 8 :], pltpu.roll(high, 1, 1), high)[:, 7:8, :]

        @pl.when(has[2][0])
        def _():
            t = p[:, :, :128]
            sz[ch, 0] = pack(jnp.where(red[:, :, :128], pltpu.roll(t, 127, 2), t), 0)

        @pl.when(has[2][1])
        def _():
            t = p[:, :, Z - 128 :]
            sz[ch, 1] = pack(jnp.where(red[:, :, Z - 128 :], pltpu.roll(t, 1, 2), t), 127)

    def start(ch, parity, edge_parity):
        if edge_parity is not None:
            for e, a, b in edges:

                @pl.when(has_edge(e, a, b))
                def _():
                    edge_copy(ch, e, a, b, edge_parity).start()

        for d, side in faces:

            @pl.when(has[d][side])
            def _():
                face_copy(ch, d, side, parity).start()

    def finish(ch, parity, edge_parity):
        for d, side in faces:

            @pl.when(has[d][side])
            def _():
                face_copy(ch, d, side, parity, True).wait_recv()
                face_copy(ch, d, side, parity).wait_send()

        if edge_parity is not None:
            finish_edges(ch, edge_parity)

    def finish_edges(ch, edge_parity):
        for e, a, b in edges:

            @pl.when(has_edge(e, a, b))
            def _():
                edge_copy(ch, e, a, b, edge_parity, True).wait_recv()
                edge_copy(ch, e, a, b, edge_parity).wait_send()

    def columns(packed, xs):
        return jnp.stack(
            [jnp.broadcast_to(packed[:, x : x + 1], (packed.shape[0], 128)) for x in xs], axis=0
        )

    near_y = sub_y < 4
    near_z = lane_z < 64

    def edge_tiles(ch):
        yz = []
        for side in range(2):
            rows8 = jnp.where(near_y[0, :, :128], hyz[ch, 1, side], hyz[ch, 0, side])
            yz.append(columns(rows8, range(X)))
        sides = []
        for side in range(2):
            xy = jnp.where(
                near_y[0],
                jnp.broadcast_to(hxy[ch, side, 1], (8, Z)),
                jnp.broadcast_to(hxy[ch, side, 0], (8, Z)),
            )
            at = 0 if side else X - 1
            xz = jnp.where(
                near_z[0],
                columns(hxz[ch, side, 1], (at,))[0],
                columns(hxz[ch, side, 0], (at,))[0],
            )
            sides.append((xy, xz))
        return jnp.where(near_z[:, :8], yz[1], yz[0]), sides

    def widen(p, ch, with_edges, second=None):
        y_plus = jnp.broadcast_to(hy[ch, 1], (X, 8, Z))
        y_minus = jnp.broadcast_to(hy[ch, 0], (X, 8, Z))
        z_plus = columns(hz[ch, 1], range(X))
        z_minus = columns(hz[ch, 0], range(X))
        if second is None:
            ytile = jnp.where(near_y, y_plus, y_minus)
            ztile = jnp.where(near_z, z_plus, z_minus)
        else:
            y_plus2 = jnp.broadcast_to(hy[second, 1], (X, 8, Z))
            y_minus2 = jnp.broadcast_to(hy[second, 0], (X, 8, Z))
            z_plus2 = columns(hz[second, 1], range(X))
            z_minus2 = columns(hz[second, 0], range(X))
            ytile = jnp.where(
                near_y,
                jnp.where(sub_y == 0, y_plus, y_plus2),
                jnp.where(sub_y == 7, y_minus, y_minus2),
            )
            ztile = jnp.where(
                near_z,
                jnp.where(lane_z == 0, z_plus, z_plus2),
                jnp.where(lane_z == 127, z_minus, z_minus2),
            )
        if with_edges:
            yztile, sides = edge_tiles(ch)
        else:
            yztile = jnp.zeros((X, 8, 128), jnp.float32)
        top = jnp.concatenate([p, ztile], axis=2)
        core = jnp.concatenate([top, jnp.concatenate([ytile, yztile], axis=2)], axis=1)
        planes = []
        for side in range(2):
            if with_edges:
                xy, xz = sides[side]
            else:
                xy = jnp.zeros((8, Z), jnp.float32)
                xz = jnp.zeros((Y, 128), jnp.float32)
            first = jnp.concatenate([hx[ch, side], xz], axis=1)
            last = jnp.concatenate([xy, jnp.zeros((8, 128), jnp.float32)], axis=1)
            planes.append(jnp.concatenate([first, last], axis=0)[None])
        return jnp.concatenate([planes[0], core, planes[1]], axis=0)

    line_of = lax.broadcasted_iota(jnp.int32, wide[1:], 0)
    cell_of = lax.broadcasted_iota(jnp.int32, wide[1:], 1)
    odd = ((line_of + cell_of) & 1) == 1
    reds = (odd, jnp.logical_not(odd))

    def around(v, low, high):
        return (
            high,
            low,
            pltpu.roll(v, Y + 7, 0),
            pltpu.roll(v, 1, 0),
            pltpu.roll(v, Z + 127, 1),
            pltpu.roll(v, 1, 1),
        )

    inner_y, outer_y = slice(0, Y), slice(Y, Y + 8)
    inner_z, outer_z = slice(0, Z), slice(Z, Z + 128)

    def region(field, i, ys, zs):
        besides = (
            field[min(i + 1, X + 1), ys, zs],
            field[max(i - 1, 0), ys, zs],
            pltpu.roll(field[i, :, zs], Y + 7, 0)[ys],
            pltpu.roll(field[i, :, zs], 1, 0)[ys],
            pltpu.roll(field[i, ys, :], Z + 127, 1)[:, zs],
            pltpu.roll(field[i, ys, :], 1, 1)[:, zs],
        )
        u = srd[i, ys, zs]
        for k, one in enumerate(besides):
            u = u + wts[k, i, ys, zs] * one
        return u

    def own_plane(field, i):
        return region(field, i, inner_y, inner_z)

    def red_region(i, ys, zs):
        after[i, ys, zs] = jnp.where(
            reds[i % 2][ys, zs], region(field, i, ys, zs), field[i, ys, zs]
        )

    def black_update():
        return jnp.stack(
            [
                jnp.where(reds[i % 2][:Y, :Z], after[i, :Y, :Z], own_plane(after, i))
                for i in range(1, X + 1)
            ],
            axis=0,
        )

    def sweep(p, ch, parity, edge_parity):
        finish(ch, parity, None)
        field[...] = widen(p, ch, False)
        for i in range(1, X + 1):
            red_region(i, inner_y, inner_z)
        finish_edges(ch, edge_parity)
        yztile, planes = edge_tiles(ch)
        field[1 : X + 1, Y : Y + 8, Z : Z + 128] = yztile
        for side in range(2):
            field[side * (X + 1), Y : Y + 8, :Z] = planes[side][0]
            field[side * (X + 1), :Y, Z : Z + 128] = planes[side][1]
        for i in (0, X + 1):
            red_region(i, inner_y, inner_z)
        for i in range(1, X + 1):
            red_region(i, outer_y, inner_z)
            red_region(i, inner_y, outer_z)
        return black_update()

    def gather_copy(buf, staged, which, off):
        return pltpu.make_async_remote_copy(
            src_ref=staged,
            dst_ref=buf.at[here[2]],
            send_sem=g_send.at[which, off - 1],
            recv_sem=g_recv.at[which, off - 1],
            device_id={"gz": lax.rem(here[2] + off, n_gz)},
            device_id_type=MESH,
        )

    def gather_start(buf, staged, which, value):
        staged[...] = value
        for off in range(1, n_gz):
            gather_copy(buf, staged, which, off).start()
        buf[here[2]] = value

    def gather_wait(buf, staged, which):
        for off in range(1, n_gz):
            gather_copy(buf, staged, which, off).wait_recv()
        return jnp.concatenate([buf[j] for j in range(n_gz)], axis=1)

    def pool(v):
        for h in range(2):
            part = v[:, :, 128 * h : 128 * h + 128].reshape(X // 2, 2, Y, 128)
            tmp[h] = (part[:, 0] + part[:, 1]).reshape(X // 2 * Y, 128)
        rows = X // 2 * Y // 2
        halves = [
            tmp[h, pl.ds(0, rows, stride=2), :] + tmp[h, pl.ds(1, rows, stride=2), :]
            for h in range(2)
        ]
        return exact_dot(jnp.concatenate(halves, axis=1), pool_m[...]) * 0.125

    loads[0].wait()
    loads[1].wait()
    c = con[...] * jnp.where(msk[...] > 0, clog_factor, 1.0)
    stage_layer(0, c, 0)
    stage_layer(1, c, 1)
    loads[2].wait()
    loads[3].wait()
    stage_layer(2, src[...], 0)
    pl.semaphore_wait(barrier, greeted)
    start(0, 0, 0)

    k_of = lax.broadcasted_iota(jnp.int32, (Z, ZC), 0)
    j_of = lax.broadcasted_iota(jnp.int32, (Z, ZC), 1)
    pool_m[...] = jnp.where((k_of >> 1) == j_of, 1.0, 0.0).astype(jnp.bfloat16)
    k_of = lax.broadcasted_iota(jnp.int32, (ZC, Z), 1)
    j_of = lax.broadcasted_iota(jnp.int32, (ZC, Z), 0)
    prol_m[...] = jnp.where((k_of >> 1) == j_of, 1.0, 0.0).astype(jnp.bfloat16)
    gather_start(cond_all, cond_send, 0, pool(c))

    rows = X // 2 * Y // 2
    col = lax.broadcasted_iota(jnp.int32, (rows, ids.shape[3]), 0)
    hit = jnp.zeros((rows, ids.shape[3]), jnp.float32)
    for o in range(ids.shape[2]):
        hit = jnp.maximum(hit, jnp.where(ids[0, 0, o : o + 1, :] == col, 1.0, 0.0))
    flag = jnp.max(hit, axis=1, keepdims=True)

    finish(0, 0, 0)
    field[...] = widen(c, 0, True, 1)
    after[...] = widen(src[...], 2, False)
    second = [
        jnp.concatenate(
            [
                jnp.concatenate([hx[1, side], jnp.zeros((Y, 128), jnp.float32)], axis=1),
                jnp.zeros((8, Z + 128), jnp.float32),
            ],
            axis=0,
        )
        for side in range(2)
    ]
    for i in range(X + 2):
        v = field[i]
        low = field[i - 1] if i else second[0]
        high = field[i + 1] if i < X + 1 else second[1]
        w = [0.5 * (v + one) for one in around(v, low, high)]
        dg = shift_fine + w[0] + w[1] + w[2] + w[3] + w[4] + w[5]
        rd = jnp.where(v > 0.0, 1.0 / dg, 0.0)
        if 0 < i < X + 1:
            diag[i - 1] = dg[:Y, :Z]
        for k in range(6):
            wts[k, i] = w[k] * rd
        v = after[i] * rd
        srd[i] = v
        after[i] = jnp.where(reds[i % 2], v, 0.0)
    p = black_update()
    stage_black(3, p)
    start(3, 1, 1)

    def factor(state, stage):
        lower, main, upper = state
        stride = 1 << stage
        rm = 1.0 / main
        low = -lower * pltpu.roll(rm, stride, 1)
        high = -upper * pltpu.roll(rm, length - stride, 1)
        fac[2 * stage] = low
        fac[2 * stage + 1] = high
        main = (
            main + low * pltpu.roll(upper, stride, 1) + high * pltpu.roll(lower, length - stride, 1)
        )
        lower = low * pltpu.roll(lower, stride, 1)
        upper = high * pltpu.roll(upper, length - stride, 1)
        return lower, main, upper

    cond = gather_wait(cond_all, cond_send, 0)
    at = lax.broadcasted_iota(jnp.int32, cond.shape, 1)
    sum_low = cond + pltpu.roll(cond, 1, 1)
    sum_high = cond + pltpu.roll(cond, length - 1, 1)
    left_sum = jnp.where(at == 0, cond, sum_low)
    right_sum = jnp.where(at == length - 1, cond, sum_high)
    state = (
        jnp.where(at == 0, 0.0, -sum_low),
        1.0 / (CZ * CZ) + left_sum + right_sum,
        jnp.where(at == length - 1, 0.0, -sum_high),
    )
    per = stages // 2
    for stage in range(0, per):
        state = factor(state, stage)
    p = sweep(p, 3, 1, 1)
    stage_black(4, p)
    start(4, 0, None)
    for stage in range(per, stages):
        state = factor(state, stage)
    fac[2 * stages] = (2.0 / (CZ * CZ)) / state[1]
    finish(4, 0, None)
    after[...] = widen(p, 4, False)
    residual = jnp.stack(
        [
            jnp.where(
                reds[i % 2][:Y, :Z],
                diag[i - 1] * (own_plane(after, i) - after[i, :Y, :Z]),
                0.0,
            )
            for i in range(1, X + 1)
        ],
        axis=0,
    )
    rhs = pool(residual) * flag
    gather_start(rhs_all, rhs_send, 1, rhs)
    values = gather_wait(rhs_all, rhs_send, 1)
    for stage in range(stages):
        stride = 1 << stage
        values = (
            values
            + fac[2 * stage] * pltpu.roll(values, stride, 1)
            + fac[2 * stage + 1] * pltpu.roll(values, length - stride, 1)
        )
    rhs_all[...] = jnp.stack(
        [
            (values * fac[2 * stages])[:, ZC * j : ZC * j + ZC]
            for j in range(n_gz)
        ],
        axis=0,
    )
    mine = rhs_all[here[2]]
    fine = exact_dot(mine, prol_m[...])
    for h in range(2):
        part = fine[:, 128 * h : 128 * h + 128]
        tmp[h, pl.ds(0, rows, stride=2), :] = part
        tmp[h, pl.ds(1, rows, stride=2), :] = part
    add = jnp.concatenate([tmp[0], tmp[1]], axis=1).reshape(X // 2, 1, Y, Z)
    p = p + jnp.broadcast_to(add, (X // 2, 2, Y, Z)).reshape(X, Y, Z)

    stage_black(5, p)
    start(5, 1, 0)
    p = sweep(p, 5, 1, 0)
    stage_black(6, p)
    start(6, 0, 1)
    out_ref[...] = sweep(p, 6, 0, 1)

    for off in range(1, n_gz):
        gather_copy(cond_all, cond_send, 0, off).wait_send()
        gather_copy(rhs_all, rhs_send, 1, off).wait_send()


def shards(sizes, source, conduct, solid_mask, line_ids):
    X, Y, Z = source.shape
    ZC = Z // 2
    rows = X // 2 * Y // 2
    n_gz = sizes[2]
    length = n_gz * ZC
    stages = (length - 1).bit_length()
    f32 = jnp.float32
    V = pltpu.VMEM
    dma = pltpu.SemaphoreType.DMA
    return pl.pallas_call(
        functools.partial(kernel, sizes),
        out_shape=jax.ShapeDtypeStruct((X, Y, Z), f32),
        in_specs=[pl.BlockSpec(memory_space=pltpu.HBM)] * 4,
        out_specs=pl.BlockSpec(memory_space=pltpu.VMEM),
        scratch_shapes=[
            V((X, Y, Z), f32),
            V((X, Y, Z), f32),
            V((X, Y, Z), jnp.int32),
            V(line_ids.shape, jnp.int32),
            V((CHANNELS, 2, Y, Z), f32),
            V((CHANNELS, 2, X, 1, Z), f32),
            V((CHANNELS, 2, Y, 128), f32),
            V((CHANNELS, 2, Y, Z), f32),
            V((CHANNELS, 2, X, 1, Z), f32),
            V((CHANNELS, 2, Y, 128), f32),
            V((CHANNELS, 2, 2, 1, Z), f32),
            V((CHANNELS, 2, 2, Y, 128), f32),
            V((CHANNELS, 2, 2, 8, 128), f32),
            V((6, X + 2, Y + 8, Z + 128), f32),
            V((X + 2, Y + 8, Z + 128), f32),
            V((X + 2, Y + 8, Z + 128), f32),
            V((X, Y, Z), f32),
            V((X + 2, Y + 8, Z + 128), f32),
            V((2, X // 2 * Y, 128), f32),
            V((Z, ZC), jnp.bfloat16),
            V((ZC, Z), jnp.bfloat16),
            V((n_gz, rows, ZC), f32),
            V((n_gz, rows, ZC), f32),
            V((rows, ZC), f32),
            V((rows, ZC), f32),
            V((2 * stages + 1, rows, length), f32),
            dma((4,)),
            dma((18,)),
            dma((2, 18)),
            dma((2, n_gz - 1)),
            dma((2, n_gz - 1)),
        ],
        compiler_params=pltpu.CompilerParams(
            collective_id=0, has_side_effects=True, vmem_limit_bytes=67043328
        ),
        name="cycle",
    )(source, conduct, solid_mask, line_ids)


def solution(mesh):
    sizes = tuple(mesh.shape[a] for a in AXES)
    in_specs = (
        P("gx", "gy", "gz"),
        P("gx", "gy", "gz"),
        P("gx", "gy", "gz"),
        P("gx", "gy", None, None),
    )
    out_specs = P("gx", "gy", "gz")
    return jax.shard_map(
        functools.partial(shards, sizes),
        mesh=mesh,
        in_specs=in_specs,
        out_specs=out_specs,
        check_vma=False,
    )
```
